512 devices in a mesh: blk: 128 (over x, y, z_lo, core), rep: 4 (over z_hi).
Axes of the slice: x: 4, y: 8, z: 8 (z_hi: 4, z_lo: 2; z = z_hi * 2 + z_lo), core: 2. Of those that a mesh axis runs over, the one named last changes fastest.
Arguments:
- image: bfloat16 [65536, 1024], P(('blk', 'rep')), may hold values from -100 to 100
- text: bfloat16 [65536, 1024], P(('blk', 'rep')), may hold values from -100 to 100
- positive: int32 [128, 512], P('blk', 'rep'), may hold values from 0 to 511, each once within a row
- logit_scale: float32 [1], replicated, may hold values from 85 to 270
Outputs:
- row_loss: float32 [65536], P(('blk', 'rep'))
- col_loss: float32 [65536], P(('blk', 'rep'))
- img_grad: float32 [65536, 1024], P(('blk', 'rep'))
- txt_grad: float32 [65536, 1024], P(('blk', 'rep'))
The draws below stay inside these ranges and needn't reach their ends.
Inputs may be any that keep to these rules, and one draw needn't show every extreme that they name: Each row of positive names every index of its block once.
All inputs are finite; a program needn't handle non-finite values.
Results may differ from the reference program's by a relative error of at most 0.0081.
The reference program's roundings to bfloat16 on the way count: a program that leaves them out, or rounds other values in their place, can miss the bound.
Values may be sent and summed in bfloat16 or wider, within the bound.
A program may use at most 64 MiB of HBM per device.

```python
import jax
import jax.numpy as jnp
from jax import lax

D = 1024
STEPS = 4
BLOCK = 512
BLOCKS = 128
PAIRS = 65536


def embed_pair(key):
    base = jax.random.fold_in(key, 7771)
    key_img, key_txt = jax.random.split(base, 2)
    image = jax.random.truncated_normal(key_img, -6.0, 6.0, (PAIRS, D), jnp.float32)
    text = jax.random.truncated_normal(key_txt, -6.0, 6.0, (PAIRS, D), jnp.float32)
    return (image, text)


def draw_image(key, part):
    return embed_pair(key)[0].astype(jnp.bfloat16)


def draw_text(key, part):
    return embed_pair(key)[1].astype(jnp.bfloat16)


def draw_logit_scale(key, part):
    inner = jax.random.fold_in(key, 55)
    return jax.random.uniform(inner, (1,), jnp.float32, 85.0, 100.0)


def setup_inputs(seed: int = 0) -> dict:
    splits = jax.random.split(jax.random.key(seed), 5)
    image = draw_image(jax.random.fold_in(splits[4], 71), 0)
    text = draw_text(jax.random.fold_in(splits[4], 71), 0)
    positive = jax.vmap(lambda own: jax.random.permutation(own, BLOCK))(jax.random.split(splits[2], BLOCKS)).reshape((BLOCKS, BLOCK)).astype(jnp.int32)
    logit_scale = draw_logit_scale(jax.random.fold_in(splits[4], 71), 0)
    return {"image": image, "text": text, "positive": positive, "logit_scale": logit_scale}


exact_mode = lax.Precision.HIGHEST

def normalize(values):
    widened = values.astype(jnp.float32)
    inverse = lax.rsqrt(lax.optimization_barrier(jnp.sum(widened * widened, axis=-1, keepdims=True)) + 1e-06)
    return (widened * inverse, inverse)

def merge_stats(earlier, later):
    highest = jnp.maximum(earlier[0], later[0])
    summed = earlier[1] * jnp.exp(earlier[0] - highest) + later[1] * jnp.exp(later[0] - highest)
    return (highest, summed)

def reference(image, text, positive, logit_scale):
    factor = logit_scale[0]
    img_unit, img_inverse = normalize(image)
    txt_unit, txt_inverse = normalize(text)
    img_round = lax.optimization_barrier(img_unit.astype(jnp.bfloat16))
    txt_round = lax.optimization_barrier(txt_unit.astype(jnp.bfloat16))
    img_tiles = img_round.astype(jnp.float32).reshape(BLOCKS, BLOCK, D)
    txt_tiles = txt_round.astype(jnp.float32).reshape(BLOCKS, BLOCK, D)
    columns = jnp.arange(BLOCK, dtype=jnp.int32)
    onehot = (positive[:, :, None] == columns[None, None, :]).astype(jnp.float32)

    def scores_at(offset):
        moved = jnp.roll(txt_tiles, offset, axis=0)
        return (moved, factor * jnp.einsum('bid,bjd->bij', img_tiles, moved, precision=exact_mode))
    for offset in range(STEPS):
        moved, scores = scores_at(offset)
        row_peak = lax.optimization_barrier(jnp.max(scores, axis=2))
        col_peak = lax.optimization_barrier(jnp.max(scores, axis=1))
        col_part = lax.optimization_barrier(jnp.sum(jnp.exp(scores - col_peak[:, None, :]), axis=1))
        col_peak = jnp.roll(col_peak, -offset, axis=0)
        col_part = jnp.roll(col_part, -offset, axis=0)
        if offset == 0:
            row_max = row_peak
            row_sum = lax.optimization_barrier(jnp.sum(jnp.exp(scores - row_peak[:, :, None]), axis=2))
            row_pos = lax.optimization_barrier(jnp.sum(onehot * scores, axis=2))
            col_pos = lax.optimization_barrier(jnp.sum(onehot * scores, axis=1))
            col_max, col_sum = (col_peak, col_part)
        else:
            highest = jnp.maximum(row_max, row_peak)
            row_sum = row_sum * jnp.exp(row_max - highest) + lax.optimization_barrier(jnp.sum(jnp.exp(scores - highest[:, :, None]), axis=2))
            row_max = highest
            col_max, col_sum = merge_stats((col_max, col_sum), (col_peak, col_part))
    row_lse = row_max + jnp.log(row_sum)
    col_lse = col_max + jnp.log(col_sum)
    img_sum = jnp.zeros((BLOCKS, BLOCK, D), jnp.float32)
    txt_sum = jnp.zeros((BLOCKS, BLOCK, D), jnp.float32)
    for offset in range(STEPS):
        moved, scores = scores_at(offset)
        col_here = jnp.roll(col_lse, offset, axis=0)
        weight = 0.5 * (jnp.exp(scores - row_lse[:, :, None]) + jnp.exp(scores - col_here[:, None, :]))
        if offset == 0:
            weight = weight - onehot
        weight = lax.optimization_barrier(weight.astype(jnp.bfloat16)).astype(jnp.float32)
        img_sum = img_sum + jnp.einsum('bij,bjd->bid', weight, moved, precision=exact_mode)
        txt_terms = jnp.einsum('bij,bid->bjd', weight, img_tiles, precision=exact_mode)
        txt_sum = txt_sum + jnp.roll(txt_terms, -offset, axis=0)
    img_sum = factor * img_sum.reshape(PAIRS, D)
    txt_sum = factor * txt_sum.reshape(PAIRS, D)
    img_grad = (img_sum - img_unit * lax.optimization_barrier(jnp.sum(img_unit * img_sum, axis=-1, keepdims=True))) * img_inverse
    txt_grad = (txt_sum - txt_unit * lax.optimization_barrier(jnp.sum(txt_unit * txt_sum, axis=-1, keepdims=True))) * txt_inverse
    row_loss = (row_lse - row_pos).reshape(PAIRS)
    col_loss = (col_lse - col_pos).reshape(PAIRS)
    return (row_loss, col_loss, img_grad, txt_grad)
```

```python
import functools

import jax
import jax.numpy as jnp
from jax import lax
from jax.experimental import pallas as pl
from jax.experimental.pallas import tpu as pltpu
from jax.sharding import PartitionSpec as P

MESH = pl.DeviceIdType.MESH
F32 = jnp.float32
BF16 = jnp.bfloat16
ROWS = 128
HALF = 64
RING = 8
LOW = -1e30


def unit_of(values):
    widened = values.astype(F32)
    inverse = lax.rsqrt(jnp.sum(widened * widened, axis=-1, keepdims=True) + 1e-06)
    return widened * inverse, inverse


def dot(a, b, dims):
    return lax.dot_general(a, b, (dims, ((), ())), preferred_element_type=F32)


def kernel(
    columns,
    scale_ref, img_ref, txt_ref, pos_ref,
    row_ref, col_ref, igrad_ref, tgrad_ref,
    texts, images, scores, weights, terms, img_acc,
    peak, part, row_hit,
    row_stat, row_got, col_stat, col_got, row_lse, col_lse, row_wide,
    sums_out, sums_in, img_out, img_in,
    txt_send, txt_recv, pic_send, pic_recv, rs_send, rs_recv, cs_send, cs_recv,
    sum_send, sum_recv, ig_send, ig_recv,
):
    blk, rep = lax.axis_index("blk"), lax.axis_index("rep")
    core = lax.rem(blk, 2)
    odd = lax.rem(lax.div(blk, 2), 2)
    col = lax.div(blk, 4)
    z = 2 * rep + odd
    factor = scale_ref[0]

    def device(column, height, which):
        return (4 * column + 2 * lax.rem(height, 2) + which, lax.div(height, 2))

    def ring(by):
        return lax.rem(z + by + RING, RING)

    def slot(height):
        return 4 * lax.rem(height, 2) + lax.div(height, 2)

    up, down = lax.rem(col + 1, columns), lax.rem(col + columns - 1, columns)
    mate = device(col, z, 1 - core)
    ups = [device(up, z, c) for c in (0, 1)]
    downs = [device(down, z, c) for c in (0, 1)]
    rings = [device(col, ring(r), core) for r in range(1, RING)]

    barrier = pltpu.get_barrier_semaphore()
    friends = [mate, *ups, *downs, *rings]
    for friend in friends:
        pl.semaphore_signal(barrier, inc=1, device_id=friend, device_id_type=MESH)

    even_from = ROWS * core * (1 - odd)
    odd_from = jnp.where(odd == 0, 2 * ROWS, ROWS * core)
    starts = (
        pl.multiple_of(jnp.where(odd == 0, even_from, odd_from), ROWS),
        pl.multiple_of(jnp.where(odd == 0, odd_from, even_from), ROWS),
    )

    img_unit, _ = unit_of(img_ref[...])
    images[core] = img_unit.astype(BF16)
    txt_unit, _ = unit_of(txt_ref[...])
    texts[slot(z)] = txt_unit.astype(BF16)

    pl.semaphore_wait(barrier, len(friends))

    def text_copy(way, depth, half):
        place = slot(ring(-depth if way == 0 else depth))
        part_of = texts.at[place, pl.ds(half * HALF, HALF)]
        to = device(col, ring(1 if way == 0 else -1), core)
        return pltpu.make_async_remote_copy(
            src_ref=part_of, dst_ref=part_of,
            send_sem=txt_send.at[way, depth, half], recv_sem=txt_recv.at[way, depth, half],
            device_id=to, device_id_type=MESH,
        )

    def text_arrival(way, depth, half):
        place = slot(ring(-depth if way == 0 else depth))
        part_of = texts.at[place, pl.ds(half * HALF, HALF)]
        return pltpu.make_async_remote_copy(
            src_ref=part_of, dst_ref=part_of,
            send_sem=txt_send.at[way, depth - 1, half], recv_sem=txt_recv.at[way, depth - 1, half],
            device_id=mate, device_id_type=MESH,
        )

    sent = []

    def start(copy):
        copy.start()
        sent.append(copy)

    for half in (0, 1):
        start(text_copy(0, 0, half))
        start(text_copy(1, 0, 1 - half))

    def image_copy(which, to, there):
        return pltpu.make_async_remote_copy(
            src_ref=images.at[core], dst_ref=images.at[there],
            send_sem=pic_send.at[which], recv_sem=pic_recv.at[which],
            device_id=to, device_id_type=MESH,
        )

    def image_arrival(which, there):
        return pltpu.make_async_remote_copy(
            src_ref=images.at[there], dst_ref=images.at[there],
            send_sem=pic_send.at[which], recv_sem=pic_recv.at[which],
            device_id=mate, device_id_type=MESH,
        )

    start(image_copy(0, mate, core))
    start(image_copy(1, device(down, z, core), 2 + core))
    start(image_copy(2, device(down, z, 1 - core), 2 + core))

    positive = jnp.broadcast_to(pos_ref[...].astype(F32), (ROWS, ROWS)).T.astype(jnp.int32)
    lanes = lax.broadcasted_iota(jnp.int32, (ROWS, ROWS), 1)
    peak[...] = jnp.full(peak.shape, LOW, F32)
    part[...] = jnp.zeros(part.shape, F32)
    row_hit[...] = jnp.zeros(row_hit.shape, F32)
    col_stat[...] = jnp.zeros(col_stat.shape, F32)
    row_stat[0] = jnp.full((8, ROWS), LOW, F32)
    row_stat[1] = jnp.zeros((8, ROWS), F32)

    def number(step):
        return 2 * abs(step) - (1 if step < 0 or step == 4 else 0)

    def score(step):
        height = ring(step)
        kind = abs(step) % 2
        first = lax.div(starts[kind], ROWS)
        left = images[pl.ds(first, 2)].reshape(2 * ROWS, -1)
        value = factor * dot(left, texts[slot(height)], ((1,), (1,)))
        scores[number(step)] = value
        old = peak[kind]
        top = jnp.maximum(old, value)
        part[kind] = part[kind] * jnp.exp(old - top) + jnp.exp(value - top)
        peak[kind] = top
        highest = jnp.max(value, axis=0, keepdims=True)
        col_stat[0, pl.ds(height, 1), :] = highest
        col_stat[1, pl.ds(height, 1), :] = jnp.sum(jnp.exp(value - highest), axis=0, keepdims=True)
        if kind == 0:
            hit = jnp.where(hits(height), value[:ROWS], 0.0)
            row_hit[...] += hit
            col_stat[2, pl.ds(height, 1), :] = jnp.sum(hit, axis=0, keepdims=True)

    def hits(height):
        return positive == lanes + ROWS * lax.div(height, 2)

    def pass_on(depth):
        for turn in (0, 1):
            for way in (0, 1):
                half = turn if way == 0 else 1 - turn
                if depth < 4 or turn == 0:
                    text_arrival(way, depth, half).wait_recv()
                    if depth < 3 or (depth == 3 and turn == 0):
                        start(text_copy(way, depth, half))

    pass_on(1)
    pass_on(2)
    image_arrival(0, 1 - core).wait_recv()
    image_arrival(1, 2 + core).wait_recv()
    image_arrival(2, 3 - core).wait_recv()
    for step in (0, -1, 1, -2, 2):
        score(step)
    pass_on(3)
    score(-3)
    score(3)
    pass_on(4)
    score(4)

    for kind in (0, 1):
        for side in (0, 1):
            tops = peak[kind, side * ROWS : (side + 1) * ROWS, :].T
            parts = part[kind, side * ROWS : (side + 1) * ROWS, :].T
            top = jnp.max(tops, axis=0, keepdims=True)
            total = jnp.sum(parts * jnp.exp(tops - top), axis=0, keepdims=True)
            at = pl.ds(lax.div(starts[kind], ROWS) + side, 1)
            old_top, old_total = row_stat[0, at, :], row_stat[1, at, :]
            new_top = jnp.maximum(old_top, top)
            row_stat[0, at, :] = new_top
            row_stat[1, at, :] = old_total * jnp.exp(old_top - new_top) + total * jnp.exp(top - new_top)

    def row_copy(which, to, there):
        return pltpu.make_async_remote_copy(
            src_ref=row_stat, dst_ref=row_got.at[there],
            send_sem=rs_send.at[which], recv_sem=rs_recv.at[there],
            device_id=to, device_id_type=MESH,
        )

    start(row_copy(0, mate, 0))
    for c in (0, 1):
        start(row_copy(1 + c, downs[c], 1 + core))
        start(row_copy(3 + c, ups[c], 3 + core))

    def col_copy(by):
        return pltpu.make_async_remote_copy(
            src_ref=col_stat, dst_ref=col_got.at[z],
            send_sem=cs_send.at[by], recv_sem=cs_recv.at[by],
            device_id=device(col, ring(by), core), device_id_type=MESH,
        )

    def col_arrival(by):
        there = col_got.at[ring(-by)]
        return pltpu.make_async_remote_copy(
            src_ref=there, dst_ref=there,
            send_sem=cs_send.at[by], recv_sem=cs_recv.at[by],
            device_id=mate, device_id_type=MESH,
        )

    for by in (4, 3, 5, 2, 6, 1, 7):
        start(col_copy(by))
    col_got[z] = col_stat[...]

    for there in range(5):
        pltpu.make_async_remote_copy(
            src_ref=row_got.at[there], dst_ref=row_got.at[there],
            send_sem=rs_send.at[0], recv_sem=rs_recv.at[there],
            device_id=mate, device_id_type=MESH,
        ).wait_recv()
    for place in range(4):
        found = [(row_stat[0, place : place + 1, :], row_stat[1, place : place + 1, :])]
        others = (0, 3, 4) if place < 2 else (0, 1, 2)
        for there in others:
            row = place if there == 0 else (place + 2) % 4
            found.append((row_got[there, 0, row : row + 1, :], row_got[there, 1, row : row + 1, :]))
        top = functools.reduce(jnp.maximum, [f[0] for f in found])
        total = functools.reduce(jnp.add, [f[1] * jnp.exp(f[0] - top) for f in found])
        lse = top + jnp.log(total)
        row_lse[place : place + 1, :] = lse
        row_wide[place] = jnp.broadcast_to(lse, (ROWS, ROWS)).T

    for by in range(1, RING):
        col_arrival(by).wait_recv()
    top = functools.reduce(jnp.maximum, [col_got[i, 0] for i in range(RING)])
    total = functools.reduce(jnp.add, [col_got[i, 1] * jnp.exp(col_got[i, 0] - top) for i in range(RING)])
    hit_sum = functools.reduce(jnp.add, [col_got[i, 2] for i in range(RING)])
    col_lse[0] = top + jnp.log(total)
    col_lse[1] = hit_sum

    def weigh(step):
        height = ring(step)
        kind = abs(step) % 2
        first = lax.div(starts[kind], ROWS)
        value = scores[number(step)]
        rows = row_wide[pl.ds(first, 2)].reshape(2 * ROWS, ROWS)
        weight = 0.5 * (jnp.exp(value - rows) + jnp.exp(value - col_lse[0, pl.ds(height, 1), :]))
        if kind == 0:
            ones = jnp.where(hits(height), 1.0, 0.0)
            weight = jnp.concatenate([weight[:ROWS] - ones, weight[ROWS:]], axis=0)
        weight = weight.astype(BF16)
        weights[kind, :, pl.ds(pl.multiple_of(ROWS * lax.div(height, 2), ROWS), ROWS)] = weight
        left = images[pl.ds(first, 2)].reshape(2 * ROWS, -1)
        terms[number(step)] = dot(weight, left, ((0,), (0,)))

    def sum_copy(way, depth, half):
        to = device(col, ring(-1 if way == 0 else 1), core)
        return pltpu.make_async_remote_copy(
            src_ref=sums_out.at[way, depth - 1, half], dst_ref=sums_in.at[way, depth - 1, half],
            send_sem=sum_send.at[way, depth - 1, half], recv_sem=sum_recv.at[way, depth - 1, half],
            device_id=to, device_id_type=MESH,
        )

    def hand_on(way, depth, half, fresh):
        step = 4 if depth == 4 else (-depth if way == 0 else depth)
        value = terms[number(step), half * HALF : (half + 1) * HALF, :]
        if not fresh:
            sum_copy(way, depth + 1, half).wait_recv()
            value = value + sums_in[way, depth, half].astype(F32)
        sums_out[way, depth - 1, half] = value.astype(BF16)
        start(sum_copy(way, depth, half))

    weigh(4)
    hand_on(0, 4, 0, True)
    hand_on(1, 4, 1, True)
    weigh(-3)
    hand_on(0, 3, 1, True)
    weigh(3)
    hand_on(1, 3, 0, True)
    weigh(-2)
    weigh(2)
    hand_on(0, 3, 0, False)
    hand_on(1, 3, 1, False)
    weigh(-1)
    weigh(1)
    weigh(0)

    img_acc[...] = jnp.zeros(img_acc.shape, F32)
    for kind in (0, 1):
        parity = odd if kind == 0 else 1 - odd
        first = lax.div(starts[kind], ROWS)
        right = texts[pl.ds(4 * parity, 4)].reshape(4 * ROWS, -1)
        share = dot(weights[kind], right, ((1,), (0,)))
        img_acc[pl.ds(first, 2)] += share.reshape(2, ROWS, -1)

    img_out[0] = img_acc[1 - core].astype(BF16)
    img_out[1] = img_acc[2].astype(BF16)
    img_out[2] = img_acc[3].astype(BF16)

    def grad_copy(which, to, there):
        return pltpu.make_async_remote_copy(
            src_ref=img_out.at[which], dst_ref=img_in.at[there],
            send_sem=ig_send.at[which], recv_sem=ig_recv.at[there],
            device_id=to, device_id_type=MESH,
        )

    start(grad_copy(0, mate, 0))
    start(grad_copy(1, ups[0], 1 + core))
    start(grad_copy(2, ups[1], 1 + core))

    hand_on(0, 2, 1, False)
    hand_on(1, 2, 0, False)
    hand_on(0, 2, 0, False)
    hand_on(1, 2, 1, False)
    hand_on(0, 1, 1, False)
    hand_on(1, 1, 0, False)
    hand_on(0, 1, 0, False)
    hand_on(1, 1, 1, False)

    hit_row = jnp.sum(row_hit[...].T, axis=0, keepdims=True)
    row_ref[...] = row_lse[pl.ds(core, 1), :] - hit_row
    col_ref[...] = col_lse[0, pl.ds(z, 1), :] - col_lse[1, pl.ds(z, 1), :]

    def finish(source, summed):
        unit, inverse = unit_of(source)
        summed = factor * summed
        return (summed - unit * jnp.sum(unit * summed, axis=-1, keepdims=True)) * inverse

    for there in range(3):
        pltpu.make_async_remote_copy(
            src_ref=img_in.at[there], dst_ref=img_in.at[there],
            send_sem=ig_send.at[0], recv_sem=ig_recv.at[there],
            device_id=mate, device_id_type=MESH,
        ).wait_recv()
    igrad_ref[...] = finish(
        img_ref[...],
        img_acc[core] + img_in[0].astype(F32) + img_in[1].astype(F32) + img_in[2].astype(F32),
    )

    for turn in (0, 1):
        for way in (0, 1):
            half = 1 - turn if way == 0 else turn
            sum_copy(way, 1, half).wait_recv()
    for half in (0, 1):
        at = slice(half * HALF, (half + 1) * HALF)
        total = terms[0, at, :] + sums_in[0, 0, half].astype(F32) + sums_in[1, 0, half].astype(F32)
        tgrad_ref[at, :] = finish(txt_ref[at, :], total)

    for copy in sent:
        copy.wait_send()


def on_device(image, text, positive, logit_scale, *, columns):
    width = image.shape[1]
    vmem = pl.BlockSpec(memory_space=pltpu.VMEM)
    dma = pltpu.SemaphoreType.DMA
    row_loss, col_loss, img_grad, txt_grad = pl.pallas_call(
        functools.partial(kernel, columns),
        out_shape=(
            jax.ShapeDtypeStruct((1, ROWS), F32),
            jax.ShapeDtypeStruct((1, ROWS), F32),
            jax.ShapeDtypeStruct((ROWS, width), F32),
            jax.ShapeDtypeStruct((ROWS, width), F32),
        ),
        in_specs=[pl.BlockSpec(memory_space=pltpu.SMEM), vmem, vmem, vmem],
        out_specs=(vmem,) * 4,
        scratch_shapes=[
            pltpu.VMEM((RING, ROWS, width), BF16),
            pltpu.VMEM((4, ROWS, width), BF16),
            pltpu.VMEM((RING, 2 * ROWS, ROWS), F32),
            pltpu.VMEM((2, 2 * ROWS, 4 * ROWS), BF16),
            pltpu.VMEM((RING, ROWS, width), F32),
            pltpu.VMEM((4, ROWS, width), F32),
            pltpu.VMEM((2, 2 * ROWS, ROWS), F32),
            pltpu.VMEM((2, 2 * ROWS, ROWS), F32),
            pltpu.VMEM((ROWS, ROWS), F32),
            pltpu.VMEM((2, 8, ROWS), F32),
            pltpu.VMEM((5, 2, 8, ROWS), F32),
            pltpu.VMEM((3, 8, ROWS), F32),
            pltpu.VMEM((RING, 3, 8, ROWS), F32),
            pltpu.VMEM((8, ROWS), F32),
            pltpu.VMEM((2, 8, ROWS), F32),
            pltpu.VMEM((4, ROWS, ROWS), F32),
            pltpu.VMEM((2, 4, 2, HALF, width), BF16),
            pltpu.VMEM((2, 4, 2, HALF, width), BF16),
            pltpu.VMEM((3, ROWS, width), BF16),
            pltpu.VMEM((3, ROWS, width), BF16),
            dma((2, 4, 2)), dma((2, 4, 2)),
            dma((3,)), dma((3,)),
            dma((5,)), dma((5,)),
            dma((RING,)), dma((RING,)),
            dma((2, 4, 2)), dma((2, 4, 2)),
            dma((3,)), dma((3,)),
        ],
        compiler_params=pltpu.CompilerParams(collective_id=0, has_side_effects=True),
    )(logit_scale, image, text, positive)
    return row_loss.reshape(ROWS), col_loss.reshape(ROWS), img_grad, txt_grad


def solution(mesh):
    placed = (P(("blk", "rep"), None), P(("blk", "rep"), None), P("blk", "rep"), P())
    return jax.shard_map(
        functools.partial(on_device, columns=mesh.shape["blk"] // 4),
        mesh=mesh,
        in_specs=placed,
        out_specs=(
            P(("blk", "rep")),
            P(("blk", "rep")),
            P(("blk", "rep"), None),
            P(("blk", "rep"), None),
        ),
        check_vma=False,
    )
```

```python
import functools

import jax
import jax.numpy as jnp
from jax import lax
from jax.experimental import pallas as pl
from jax.experimental.pallas import tpu as pltpu
from jax.sharding import PartitionSpec as P

MESH = pl.DeviceIdType.MESH
F32 = jnp.float32
BF16 = jnp.bfloat16
ROWS = 128
HALF = 64
RING = 8
LOW = -1e30
OWN, BEHIND, NEAR, FAR = range(4)


def unit_of(values):
    widened = values.astype(F32)
    inverse = lax.rsqrt(jnp.sum(widened * widened, axis=-1, keepdims=True) + 1e-06)
    return widened * inverse, inverse


def dot(a, b, dims):
    return lax.dot_general(a, b, (dims, ((), ())), preferred_element_type=F32)


def halves(array):
    return [array[h * HALF : (h + 1) * HALF] for h in (0, 1)]


def kernel(
    columns,
    scale_ref, img_ref, txt_ref, pos_ref,
    row_ref, col_ref, igrad_ref, tgrad_ref,
    texts, images, pos_out, pos_in, scores, weights, terms, img_acc,
    peak, part, row_hit,
    row_stat, row_got, col_stat, col_got, row_lse, col_lse, row_wide,
    back_out, back_in, near_out, near_in, mate_out, mate_in, over_out, over_in, swap_out, swap_in,
    txt_send, txt_recv, pic_send, pic_recv, rs_send, rs_recv, cs_send, cs_recv,
    back_send, back_recv, near_send, near_recv, ig_send, ig_recv,
):
    blk, rep = lax.axis_index("blk"), lax.axis_index("rep")
    core = lax.rem(blk, 2)
    odd = lax.rem(lax.div(blk, 2), 2)
    col = lax.div(blk, 4)
    z = 2 * rep + odd
    tau = 1 - 2 * odd
    factor = scale_ref[0]

    def device(column, height, which):
        return (4 * column + 2 * lax.rem(height, 2) + which, lax.div(height, 2))

    def ring(by):
        return lax.rem(z + by + 2 * RING, RING)

    up, down = lax.rem(col + 1, columns), lax.rem(col + columns - 1, columns)
    pair_z, near_z, behind_z, far_z, ahead_z = (ring(s * tau) for s in (1, -1, -2, -3, 2))
    heights = (z, behind_z, near_z, far_z)
    other = 1 - core
    mate = device(col, z, other)
    pair = device(col, pair_z, core)
    near = device(col, near_z, core)
    behind = device(col, behind_z, core)
    ahead = device(col, ahead_z, core)

    def square(column):
        return [device(column, h, c) for h in (z, pair_z) for c in (core, other)]

    row_to = [(to, n) for n, to in enumerate(square(col)[1:])]
    row_to += [(to, 7 + n) for n, to in enumerate(square(up))]
    row_to += [(to, 3 + n) for n, to in enumerate(square(down))]
    col_to = [(near, 0)]
    col_to += [(device(col, ring(by), core), n) for by, n in ((3, 4), (-3, 3), (2, 2), (-2, 1))]

    barrier = pltpu.get_barrier_semaphore()
    friends = [to for to, _ in row_to + col_to]
    for friend in friends:
        pl.semaphore_signal(barrier, inc=1, device_id=friend, device_id_type=MESH)

    own_at, pair_at = 2 * odd + core, 2 * (1 - odd) + core
    firsts = (own_at, own_at, pair_at, pair_at)
    mate_own_at, mate_pair_at = 2 * odd + other, 2 * (1 - odd) + other

    img_unit, _ = unit_of(img_ref[...])
    images[own_at] = img_unit.astype(BF16)
    txt_unit, _ = unit_of(txt_ref[...])
    texts[OWN] = txt_unit.astype(BF16)
    pos_out[...] = jnp.broadcast_to(pos_ref[...].astype(F32), (8, ROWS))

    pl.semaphore_wait(barrier, len(friends))

    sent = []

    def remote(src, dst, send, recv, to):
        return pltpu.make_async_remote_copy(
            src_ref=src, dst_ref=dst, send_sem=send, recv_sem=recv, device_id=to, device_id_type=MESH
        )

    def arrival(place, send, recv):
        return remote(place, place, send, recv, mate)

    def start(copy, given=None):
        if given is None:
            copy.start()
        else:
            pl.when(given)(copy.start)
        sent.append((copy, given))

    def arrived(copy, given=None):
        if given is None:
            copy.wait_recv()
        else:
            pl.when(given)(copy.wait_recv)

    def text_copy(kind, half):
        src, dst, to = ((OWN, NEAR, near), (OWN, BEHIND, ahead), (NEAR, FAR, ahead))[kind]
        at = pl.ds(half * HALF, HALF)
        return remote(texts.at[src, at], texts.at[dst, at], txt_send.at[kind, half], txt_recv.at[kind, half], to)

    def text_arrival(kind, half):
        place = texts.at[(NEAR, BEHIND, FAR)[kind], pl.ds(half * HALF, HALF)]
        return arrival(place, txt_send.at[kind, half], txt_recv.at[kind, half])

    def image_copy(kind, src, dst, to):
        return remote(images.at[src], images.at[dst], pic_send.at[kind], pic_recv.at[kind], to)

    def image_arrival(kind, place):
        return arrival(images.at[place], pic_send.at[kind], pic_recv.at[kind])

    below = device(down, z, core)
    own_goes, pair_goes = own_at != 3, pair_at != 3
    mate_own_goes, mate_pair_goes = mate_own_at != 3, mate_pair_at != 3

    start(text_copy(0, 0))
    start(image_copy(0, own_at, own_at, pair))
    start(text_copy(0, 1))
    start(image_copy(1, own_at, own_at, mate))
    start(image_copy(3, own_at, own_at + 4, below), own_goes)
    start(text_copy(1, 0))
    start(text_copy(1, 1))
    start(remote(pos_out, pos_in, pic_send.at[7], pic_recv.at[7], pair))

    lanes = lax.broadcasted_iota(jnp.int32, (ROWS, ROWS), 1)
    peak[...] = jnp.full(peak.shape, LOW, F32)
    part[...] = jnp.zeros(part.shape, F32)
    row_hit[...] = jnp.zeros(row_hit.shape, F32)
    row_stat[0] = jnp.full((8, ROWS), LOW, F32)
    row_stat[1] = jnp.zeros((8, ROWS), F32)
    row_stat[2] = jnp.zeros((8, ROWS), F32)
    col_stat[0] = jnp.full((8, ROWS), LOW, F32)
    col_stat[1] = jnp.zeros((8, ROWS), F32)
    col_stat[2] = jnp.zeros((8, ROWS), F32)

    for half in (0, 1):
        text_arrival(0, half).wait_recv()
        start(text_copy(2, half))
    image_arrival(0, pair_at).wait_recv()
    start(image_copy(4, pair_at, pair_at + 4, below), pair_goes)
    start(image_copy(2, pair_at, pair_at, mate))
    arrival(pos_in, pic_send.at[7], pic_recv.at[7]).wait_recv()

    def column(values):
        return jnp.broadcast_to(values, (ROWS, ROWS)).T.astype(jnp.int32)

    positive = (column(pos_out[0:1, :]), column(pos_in[0:1, :]))

    image_arrival(1, mate_own_at).wait_recv()
    image_arrival(2, mate_pair_at).wait_recv()
    arrived(image_arrival(3, own_at + 4), own_goes)
    start(image_copy(5, own_at + 4, own_at + 4, mate), own_goes)
    arrived(image_arrival(4, pair_at + 4), pair_goes)
    start(image_copy(6, pair_at + 4, pair_at + 4, mate), pair_goes)
    arrived(image_arrival(5, mate_own_at + 4), mate_own_goes)
    arrived(image_arrival(6, mate_pair_at + 4), mate_pair_goes)

    def hits(which):
        return positive[which // 2] == lanes + ROWS * lax.div(heights[which], 2)

    def window(which):
        return images[pl.ds(firsts[which], 4)].reshape(4 * ROWS, -1)

    def score(which):
        value = factor * dot(window(which), texts[which], ((1,), (1,)))
        scores[which] = value
        highest = jnp.max(value, axis=0, keepdims=True)
        at = pl.ds(heights[which], 1)
        col_stat[0, at, :] = highest
        col_stat[1, at, :] = jnp.sum(jnp.exp(value - highest), axis=0, keepdims=True)
        hit = jnp.where(hits(which), value[:ROWS], 0.0)
        row_hit[which // 2] += hit
        col_stat[2, at, :] = jnp.sum(hit, axis=0, keepdims=True)
        blocks = value.reshape(4, ROWS, ROWS)
        here = pl.ds(firsts[which], 4)
        old = peak[here]
        top = jnp.maximum(old, blocks)
        part[here] = part[here] * jnp.exp(old - top) + jnp.exp(blocks - top)
        peak[here] = top

    def row_total(place):
        tops, parts = peak[place].T, part[place].T
        top = jnp.max(tops, axis=0, keepdims=True)
        row_stat[0, pl.ds(place, 1), :] = top
        row_stat[1, pl.ds(place, 1), :] = jnp.sum(parts * jnp.exp(tops - top), axis=0, keepdims=True)

    score(OWN)
    score(NEAR)
    text_arrival(1, 0).wait_recv()
    text_arrival(1, 1).wait_recv()
    score(BEHIND)
    row_total(own_at + 2 * odd)
    row_total(own_at + 2 * odd + 1)
    row_stat[2, pl.ds(own_at, 1), :] = jnp.sum(row_hit[0].T, axis=0, keepdims=True)
    text_arrival(2, 0).wait_recv()
    text_arrival(2, 1).wait_recv()
    score(FAR)
    for n in range(4):
        row_total(pair_at + n)
    row_stat[2, pl.ds(pair_at, 1), :] = jnp.sum(row_hit[1].T, axis=0, keepdims=True)

    for to, n in row_to:
        start(remote(row_stat, row_got.at[n], rs_send.at[n], rs_recv.at[n], to))
    for to, n in col_to:
        start(remote(col_stat, col_got.at[n], cs_send.at[n], cs_recv.at[n], to))

    def total_of(found):
        top = functools.reduce(jnp.maximum, [f[0] for f in found])
        return top + jnp.log(functools.reduce(jnp.add, [f[1] * jnp.exp(f[0] - top) for f in found]))

    for n in range(11):
        arrival(row_got.at[n], rs_send.at[n], rs_recv.at[n]).wait_recv()
    found = [(row_stat[0], row_stat[1])] + [(row_got[n, 0], row_got[n, 1]) for n in range(3)]
    for n in range(4):
        found.append(
            tuple(
                jnp.concatenate([row_got[7 + n, k, 4:8, :], row_got[3 + n, k, 0:4, :]], axis=0) for k in (0, 1)
            )
        )
    row_lse[...] = total_of(found)
    for n in range(6):
        row_wide[core + n] = jnp.broadcast_to(row_lse[pl.ds(core + n, 1), :], (ROWS, ROWS)).T

    for n in range(5):
        arrival(col_got.at[n], cs_send.at[n], cs_recv.at[n]).wait_recv()
    found = [(col_stat[0], col_stat[1])] + [(col_got[n, 0], col_got[n, 1]) for n in range(5)]
    col_lse[0] = total_of(found)
    col_lse[1] = functools.reduce(jnp.add, [col_stat[2]] + [col_got[n, 2] for n in range(5)])

    def weigh(which):
        value = scores[which]
        rows = row_wide[pl.ds(firsts[which], 4)].reshape(4 * ROWS, ROWS)
        weight = 0.5 * (jnp.exp(value - rows) + jnp.exp(value - col_lse[0, pl.ds(heights[which], 1), :]))
        ones = jnp.where(hits(which), 1.0, 0.0)
        weight = jnp.concatenate([weight[:ROWS] - ones, weight[ROWS:]], axis=0).astype(BF16)
        kind, side = divmod(which, 2)
        weights[kind, :, side * ROWS : (side + 1) * ROWS] = weight
        return dot(weight, window(which), ((0,), (0,)))

    def back_copy(kind, half):
        place = (kind, half)
        return remote(back_out.at[place], back_in.at[place], back_send.at[place], back_recv.at[place], behind)

    def near_copy(half):
        return remote(near_out.at[half], near_in.at[half], near_send.at[half], near_recv.at[half], near)

    for kind, which in ((1, FAR), (0, BEHIND)):
        for half, share in enumerate(halves(weigh(which))):
            back_out[kind, half] = share.astype(BF16)
            start(back_copy(kind, half))
    terms[0] = weigh(NEAR)
    terms[1] = weigh(OWN)

    img_acc[...] = jnp.zeros(img_acc.shape, F32)
    for kind, first in ((0, own_at), (1, pair_at)):
        right = texts[2 * kind : 2 * kind + 2].reshape(2 * ROWS, -1)
        img_acc[pl.ds(first, 4)] += dot(weights[kind], right, ((1,), (0,))).reshape(4, ROWS, -1)

    def grad_copy(n, src, dst, to):
        return remote(src, dst, ig_send.at[n], ig_recv.at[n], to)

    mates = [grad_copy(k, mate_out.at[k], mate_in.at[k], mate) for k in range(3)]
    for k in (2, 1, 0):
        mate_out[k] = img_acc[core + 1 + 2 * k].astype(BF16)
        start(mates[k])
    above = device(up, z, core)
    overs = [grad_copy(3 + k, over_out.at[k], over_in.at[k], above) for k in (0, 1)]
    swap = grad_copy(5, swap_out, swap_in, pair)
    for k in (2, 1, 0):
        mates[k].wait_recv()
        img_acc[2 - core + 2 * k] += mate_in[k].astype(F32)
    for k, (place, goes) in enumerate(((pair_at, pair_goes), (own_at, own_goes))):
        over_out[k] = img_acc[4 + place].astype(BF16)
        start(overs[k], goes)

    for half in (0, 1):
        back_copy(1, half).wait_recv()
        near_out[half] = (halves(terms[0])[half] + back_in[1, half].astype(F32)).astype(BF16)
        start(near_copy(half))

    for k, (place, goes) in enumerate(((pair_at, pair_goes), (own_at, own_goes))):
        @pl.when(goes)
        def _():
            overs[k].wait_recv()
            img_acc[place] += over_in[k].astype(F32)

        if k == 0:
            swap_out[...] = img_acc[pair_at].astype(BF16)
            start(swap)

    row_ref[...] = row_lse[pl.ds(own_at, 1), :] - (
        row_stat[2, pl.ds(own_at, 1), :] + row_got[1, 2, pl.ds(own_at, 1), :]
    )
    col_ref[...] = col_lse[0, pl.ds(z, 1), :] - col_lse[1, pl.ds(z, 1), :]

    def finish(source, summed):
        unit, inverse = unit_of(source)
        summed = factor * summed
        return (summed - unit * jnp.sum(unit * summed, axis=-1, keepdims=True)) * inverse

    swap.wait_recv()
    igrad_ref[...] = finish(img_ref[...], img_acc[own_at] + swap_in[...].astype(F32))

    for half in (0, 1):
        at = slice(half * HALF, (half + 1) * HALF)
        back_copy(0, half).wait_recv()
        near_copy(half).wait_recv()
        total = terms[1, at, :] + back_in[0, half].astype(F32) + near_in[half].astype(F32)
        tgrad_ref[at, :] = finish(txt_ref[at, :], total)

    for copy, given in sent:
        if given is None:
            copy.wait_send()
        else:
            pl.when(given)(copy.wait_send)


def hand_out(row_in, col_in, igrad_in, tgrad_in, row_ref, col_ref, igrad_ref, tgrad_ref, sems):
    copies = [
        pltpu.make_async_copy(igrad_in, igrad_ref, sems.at[0]),
        pltpu.make_async_copy(tgrad_in, tgrad_ref, sems.at[1]),
    ]
    for copy in copies:
        copy.start()
    row_ref[...] = row_in[0]
    col_ref[...] = col_in[0]
    for copy in copies:
        copy.wait()


def on_device(image, text, positive, logit_scale, *, columns):
    width = image.shape[1]
    vmem = pl.BlockSpec(memory_space=pltpu.VMEM)
    dma = pltpu.SemaphoreType.DMA
    line, whole = pltpu.VMEM((1, ROWS), F32), pltpu.VMEM((ROWS, width), F32)
    found = pl.pallas_call(
        functools.partial(kernel, columns),
        out_shape=(line, line, whole, whole),
        in_specs=[pl.BlockSpec(memory_space=pltpu.SMEM), vmem, vmem, vmem],
        out_specs=(vmem,) * 4,
        scratch_shapes=[
            pltpu.VMEM((4, ROWS, width), BF16),
            pltpu.VMEM((8, ROWS, width), BF16),
            pltpu.VMEM((8, ROWS), F32),
            pltpu.VMEM((8, ROWS), F32),
            pltpu.VMEM((4, 4 * ROWS, ROWS), F32),
            pltpu.VMEM((2, 4 * ROWS, 2 * ROWS), BF16),
            pltpu.VMEM((2, ROWS, width), F32),
            pltpu.VMEM((8, ROWS, width), F32),
            pltpu.VMEM((8, ROWS, ROWS), F32),
            pltpu.VMEM((8, ROWS, ROWS), F32),
            pltpu.VMEM((2, ROWS, ROWS), F32),
            pltpu.VMEM((3, 8, ROWS), F32),
            pltpu.VMEM((11, 3, 8, ROWS), F32),
            pltpu.VMEM((3, 8, ROWS), F32),
            pltpu.VMEM((5, 3, 8, ROWS), F32),
            pltpu.VMEM((8, ROWS), F32),
            pltpu.VMEM((2, 8, ROWS), F32),
            pltpu.VMEM((8, ROWS, ROWS), F32),
            pltpu.VMEM((2, 2, HALF, width), BF16),
            pltpu.VMEM((2, 2, HALF, width), BF16),
            pltpu.VMEM((2, HALF, width), BF16),
            pltpu.VMEM((2, HALF, width), BF16),
            pltpu.VMEM((3, ROWS, width), BF16),
            pltpu.VMEM((3, ROWS, width), BF16),
            pltpu.VMEM((2, ROWS, width), BF16),
            pltpu.VMEM((2, ROWS, width), BF16),
            pltpu.VMEM((ROWS, width), BF16),
            pltpu.VMEM((ROWS, width), BF16),
            dma((3, 2)), dma((3, 2)),
            dma((8,)), dma((8,)),
            dma((11,)), dma((11,)),
            dma((5,)), dma((5,)),
            dma((2, 2)), dma((2, 2)),
            dma((2,)), dma((2,)),
            dma((6,)), dma((6,)),
        ],
        compiler_params=pltpu.CompilerParams(collective_id=0, has_side_effects=True),
    )(logit_scale, image, text, positive)
    flat = jax.ShapeDtypeStruct((ROWS,), F32)
    anywhere = pl.BlockSpec(memory_space=pl.ANY)
    found = [pltpu.with_memory_space_constraint(x, pltpu.VMEM) for x in found]
    return pl.pallas_call(
        hand_out,
        out_shape=(flat, flat, *[jax.ShapeDtypeStruct((ROWS, width), F32)] * 2),
        in_specs=[vmem] * 4,
        out_specs=(vmem, vmem, anywhere, anywhere),
        scratch_shapes=[dma((2,))],
    )(*found)


def solution(mesh):
    placed = (P(("blk", "rep"), None), P(("blk", "rep"), None), P("blk", "rep"), P())
    return jax.shard_map(
        functools.partial(on_device, columns=mesh.shape["blk"] // 4),
        mesh=mesh,
        in_specs=placed,
        out_specs=(
            P(("blk", "rep")),
            P(("blk", "rep")),
            P(("blk", "rep"), None),
            P(("blk", "rep"), None),
        ),
        check_vma=False,
    )
```

```python
import functools

import jax
import jax.numpy as jnp
from jax import lax
from jax.experimental import pallas as pl
from jax.experimental.pallas import tpu as pltpu
from jax.sharding import PartitionSpec as P

MESH = pl.DeviceIdType.MESH
F32 = jnp.float32
BF16 = jnp.bfloat16
ROWS = 128
HALF = 64
RING = 8
LOW = -1e30


def unit_of(values):
    widened = values.astype(F32)
    inverse = lax.rsqrt(jnp.sum(widened * widened, axis=-1, keepdims=True) + 1e-06)
    return widened * inverse, inverse


def dot(a, b, dims):
    return lax.dot_general(a, b, (dims, ((), ())), preferred_element_type=F32)


def halves(array):
    return [array[h * HALF : (h + 1) * HALF] for h in (0, 1)]


def kernel(
    columns,
    scale_ref, img_ref, txt_ref, pos_ref,
    row_ref, col_ref, igrad_ref, tgrad_ref,
    texts, images, pos_out, pos_in, pos_wide, scores, weights, terms, img_acc,
    peak, part, row_hit,
    row_stat, row_got, col_stat, col_got, row_lse, col_lse, row_wide,
    back_out, back_in, near_out, near_in, mate_out, mate_in, over_out, over_in, swap_out, swap_in,
    txt_send, txt_recv, pic_send, pic_recv, rs_send, rs_recv, cs_send, cs_recv,
    back_send, back_recv, near_send, near_recv, mate_send, mate_recv, over_send, over_recv, swap_send, swap_recv,
):
    blk, rep = lax.axis_index("blk"), lax.axis_index("rep")
    core = lax.rem(blk, 2)
    odd = lax.rem(lax.div(blk, 2), 2)
    col = lax.div(blk, 4)
    z = 2 * rep + odd
    tau = 1 - 2 * odd
    factor = scale_ref[0]

    def device(column, height, which):
        return (4 * column + 2 * lax.rem(height, 2) + which, lax.div(height, 2))

    def ring(by):
        return lax.rem(z + by + 2 * RING, RING)

    up, down = lax.rem(col + 1, columns), lax.rem(col + columns - 1, columns)
    pair_z, near_z, behind_z, far_z, ahead_z = (ring(s * tau) for s in (1, -1, -2, -3, 2))
    OWN, BEHIND, NEAR, FAR = 2 * odd, 2 * odd + 1, 2 - 2 * odd, 3 - 2 * odd
    is_odd = odd == 1
    other = 1 - core
    mate = device(col, z, other)
    pair = device(col, pair_z, core)
    near = device(col, near_z, core)
    behind = device(col, behind_z, core)
    ahead = device(col, ahead_z, core)

    def square(column):
        return [device(column, h, c) for h in (z, pair_z) for c in (core, other)]

    row_to = [(to, n) for n, to in enumerate(square(col)[1:])]
    row_to += [(to, 7 + n) for n, to in enumerate(square(up))]
    row_to += [(to, 3 + n) for n, to in enumerate(square(down))]
    col_to = [(near, 0)]
    col_to += [(device(col, ring(by), core), n) for by, n in ((3, 4), (-3, 3), (2, 2), (-2, 1))]

    barrier = pltpu.get_barrier_semaphore()
    friends = [to for to, _ in row_to + col_to]
    for friend in friends:
        pl.semaphore_signal(barrier, inc=1, device_id=friend, device_id_type=MESH)

    own_at, pair_at = 2 * odd + core, 2 * (1 - odd) + core
    mate_own_at, mate_pair_at = 2 * odd + other, 2 * (1 - odd) + other

    txt_unit, _ = unit_of(txt_ref[...])
    texts[OWN] = txt_unit.astype(BF16)

    pl.semaphore_wait(barrier, len(friends))

    sent = []

    def remote(src, dst, send, recv, to):
        return pltpu.make_async_remote_copy(
            src_ref=src, dst_ref=dst, send_sem=send, recv_sem=recv, device_id=to, device_id_type=MESH
        )

    def arrival(place, send, recv):
        return remote(place, place, send, recv, mate)

    def start(copy, given=None):
        if given is None:
            copy.start()
        else:
            pl.when(given)(copy.start)
        sent.append((copy, given))

    def arrived(copy, given=None):
        if given is None:
            copy.wait_recv()
        else:
            pl.when(given)(copy.wait_recv)

    def text_copy(kind, half):
        src, dst, to = ((OWN, OWN, near), (OWN, BEHIND, ahead), (NEAR, FAR, ahead))[kind]
        at = pl.ds(half * HALF, HALF)
        return remote(texts.at[src, at], texts.at[dst, at], txt_send.at[kind, half], txt_recv.at[kind, half], to)

    def text_arrival(kind, half):
        place = texts.at[(NEAR, BEHIND, FAR)[kind], pl.ds(half * HALF, HALF)]
        return arrival(place, txt_send.at[kind, half], txt_recv.at[kind, half])

    def image_copy(kind, src, dst, to):
        return remote(images.at[src], images.at[dst], pic_send.at[kind], pic_recv.at[kind], to)

    def image_arrival(kind, place):
        return arrival(images.at[place], pic_send.at[kind], pic_recv.at[kind])

    below = device(down, z, core)
    own_goes, pair_goes = own_at != 3, pair_at != 3
    mate_own_goes, mate_pair_goes = mate_own_at != 3, mate_pair_at != 3

    start(text_copy(0, 0))
    start(text_copy(0, 1))
    img_unit, _ = unit_of(img_ref[...])
    images[own_at] = img_unit.astype(BF16)
    pos_out[...] = jnp.broadcast_to(pos_ref[...].astype(F32), (8, ROWS))
    start(image_copy(0, own_at, own_at, pair))
    start(image_copy(1, own_at, own_at, mate))
    start(image_copy(3, own_at, own_at + 4, below), own_goes)
    start(text_copy(1, 0))
    start(text_copy(1, 1))
    start(remote(pos_out, pos_in, pic_send.at[7], pic_recv.at[7], pair))

    lanes = lax.broadcasted_iota(jnp.int32, (ROWS, ROWS), 1)
    peak[...] = jnp.full(peak.shape, LOW, F32)
    part[...] = jnp.zeros(part.shape, F32)
    row_hit[...] = jnp.zeros(row_hit.shape, F32)
    row_stat[0] = jnp.full((8, ROWS), LOW, F32)
    row_stat[1] = jnp.zeros((8, ROWS), F32)
    row_stat[2] = jnp.zeros((8, ROWS), F32)
    col_stat[0] = jnp.full((8, ROWS), LOW, F32)
    col_stat[1] = jnp.zeros((8, ROWS), F32)
    col_stat[2] = jnp.zeros((8, ROWS), F32)

    for half in (0, 1):
        text_arrival(0, half).wait_recv()
        start(text_copy(2, half))
    image_arrival(0, pair_at).wait_recv()
    start(image_copy(4, pair_at, pair_at + 4, below), pair_goes)
    start(image_copy(2, pair_at, pair_at, mate))
    arrival(pos_in, pic_send.at[7], pic_recv.at[7]).wait_recv()

    def column(values):
        return jnp.broadcast_to(values, (ROWS, ROWS)).T.astype(jnp.int32)

    pos_wide[odd] = column(pos_out[0:1, :])
    pos_wide[1 - odd] = column(pos_in[0:1, :])

    image_arrival(1, mate_own_at).wait_recv()
    image_arrival(2, mate_pair_at).wait_recv()
    arrived(image_arrival(3, own_at + 4), own_goes)
    start(image_copy(5, own_at + 4, own_at + 4, mate), own_goes)
    arrived(image_arrival(4, pair_at + 4), pair_goes)
    start(image_copy(6, pair_at + 4, pair_at + 4, mate), pair_goes)
    arrived(image_arrival(5, mate_own_at + 4), mate_own_goes)
    arrived(image_arrival(6, mate_pair_at + 4), mate_pair_goes)

    def hits(parity, height):
        return pos_wide[parity] == lanes + ROWS * lax.div(height, 2)

    def window(parity):
        return images[pl.ds(2 * parity + core, 4)].reshape(4 * ROWS, -1)

    def score(which, parity, height):
        value = factor * dot(window(parity), texts[which], ((1,), (1,)))
        scores[which] = value
        highest = jnp.max(value, axis=0, keepdims=True)
        at = pl.ds(height, 1)
        col_stat[0, at, :] = highest
        col_stat[1, at, :] = jnp.sum(jnp.exp(value - highest), axis=0, keepdims=True)
        hit = jnp.where(hits(parity, height), value[:ROWS], 0.0)
        row_hit[parity] += hit
        col_stat[2, at, :] = jnp.sum(hit, axis=0, keepdims=True)
        blocks = value.reshape(4, ROWS, ROWS)
        here = pl.ds(2 * parity + core, 4)
        old = peak[here]
        top = jnp.maximum(old, blocks)
        part[here] = part[here] * jnp.exp(old - top) + jnp.exp(blocks - top)
        peak[here] = top

    def row_total(place):
        logs = (peak[place] + jnp.log(part[place])).T
        top = jnp.max(logs, axis=0, keepdims=True)
        row_stat[0, pl.ds(place, 1), :] = top
        row_stat[1, pl.ds(place, 1), :] = jnp.sum(jnp.exp(logs - top), axis=0, keepdims=True)

    score(OWN, odd, z)
    score(NEAR, 1 - odd, near_z)
    text_arrival(1, 0).wait_recv()
    text_arrival(1, 1).wait_recv()
    score(BEHIND, odd, behind_z)
    row_total(own_at + 2 * odd)
    row_total(own_at + 2 * odd + 1)
    row_stat[2, pl.ds(own_at, 1), :] = jnp.sum(row_hit[odd].T, axis=0, keepdims=True)
    text_arrival(2, 0).wait_recv()
    text_arrival(2, 1).wait_recv()
    score(FAR, 1 - odd, far_z)
    for n in range(4):
        row_total(pair_at + n)
    row_stat[2, pl.ds(pair_at, 1), :] = jnp.sum(row_hit[1 - odd].T, axis=0, keepdims=True)

    for to, n in row_to:
        start(remote(row_stat, row_got.at[n], rs_send.at[n], rs_recv.at[n], to))
    for to, n in col_to:
        start(remote(col_stat, col_got.at[n], cs_send.at[n], cs_recv.at[n], to))

    def total_of(found):
        top = functools.reduce(jnp.maximum, [f[0] for f in found])
        return top + jnp.log(functools.reduce(jnp.add, [f[1] * jnp.exp(f[0] - top) for f in found]))

    for n in range(11):
        arrival(row_got.at[n], rs_send.at[n], rs_recv.at[n]).wait_recv()
    found = [(row_stat[0], row_stat[1])] + [(row_got[n, 0], row_got[n, 1]) for n in range(3)]
    for n in range(4):
        found.append(
            tuple(
                jnp.concatenate([row_got[7 + n, k, 4:8, :], row_got[3 + n, k, 0:4, :]], axis=0) for k in (0, 1)
            )
        )
    row_lse[...] = total_of(found)
    for n in range(6):
        row_wide[core + n] = jnp.broadcast_to(row_lse[pl.ds(core + n, 1), :], (ROWS, ROWS)).T

    for n in range(5):
        arrival(col_got.at[n], cs_send.at[n], cs_recv.at[n]).wait_recv()
    found = [(col_stat[0], col_stat[1])] + [(col_got[n, 0], col_got[n, 1]) for n in range(5)]
    col_lse[0] = total_of(found)
    col_lse[1] = functools.reduce(jnp.add, [col_stat[2]] + [col_got[n, 2] for n in range(5)])

    def weigh(parity, side, height):
        value = scores[2 * parity + side]
        rows = row_wide[pl.ds(2 * parity + core, 4)].reshape(4 * ROWS, ROWS)
        weight = 0.5 * (jnp.exp(value - rows) + jnp.exp(value - col_lse[0, pl.ds(height, 1), :]))
        ones = jnp.where(hits(parity, height), 1.0, 0.0)
        weight = jnp.concatenate([weight[:ROWS] - ones, weight[ROWS:]], axis=0).astype(BF16)
        weights[parity, :, side * ROWS : (side + 1) * ROWS] = weight

    def text_term(parity, side):
        weight = weights[parity, :, side * ROWS : (side + 1) * ROWS]
        return dot(weight, window(parity), ((0,), (0,)))

    def image_term(parity, part_of):
        right = texts[2 * parity : 2 * parity + 2].reshape(2 * ROWS, -1)
        left = weights[parity, part_of * 2 * ROWS : (part_of + 1) * 2 * ROWS, :]
        return dot(left, right, ((1,), (0,))).reshape(2, ROWS, -1)

    def back_copy(kind, half):
        place = (kind, half)
        return remote(back_out.at[place], back_in.at[place], back_send.at[place], back_recv.at[place], behind)

    def near_copy(half):
        return remote(near_out.at[half], near_in.at[half], near_send.at[half], near_recv.at[half], near)

    def send_back(kind, value):
        for half, share in enumerate(halves(value)):
            back_out[kind, half] = share.astype(BF16)
            start(back_copy(kind, half))

    above = device(up, z, core)
    above_even = device(up, z, 0)
    core_0, core_1 = core == 0, core == 1

    def mate_copy(n):
        return remote(mate_out.at[n], mate_in.at[n], mate_send.at[n], mate_recv.at[n], mate)

    def over_copy(kind, half):
        place = (kind, half)
        to = above if kind == 0 else above_even
        return remote(over_out.at[place], over_in.at[place], over_send.at[place], over_recv.at[place], to)

    def swap_copy(half):
        return remote(swap_out.at[half], swap_in.at[half], swap_send.at[half], swap_recv.at[half], pair)

    weigh(1 - odd, 1, far_z)
    send_back(1, text_term(1 - odd, 1))
    weigh(1 - odd, 0, near_z)
    weigh(odd, 0, z)
    weigh(odd, 1, behind_z)
    img_acc[4:6] = image_term(1, 1)
    img_acc[2:4] = image_term(1, 0) + image_term(0, 1)
    mate_out[0] = img_acc[5 - 2 * core].astype(BF16)
    start(mate_copy(0))
    for half in (0, 1):
        over_out[1, half] = img_acc[5, half * HALF : (half + 1) * HALF, :].astype(BF16)
        start(over_copy(1, half), core_1 & (odd == 0))
    mate_copy(0).wait_recv()
    for half in (0, 1):
        at = slice(half * HALF, (half + 1) * HALF)
        over_out[0, half] = (img_acc[4, at, :] + mate_in[0, at, :].astype(F32)).astype(BF16)
        start(over_copy(0, half))
    for half in (0, 1):
        start(over_copy(1, half), core_1 & is_odd)
    send_back(0, text_term(odd, 1))
    img_acc[0:2] = image_term(0, 0)
    mate_out[1] = img_acc[1].astype(BF16)
    start(mate_copy(1))
    mate_out[2] = img_acc[3].astype(BF16)
    start(mate_copy(2), core_0)
    terms[0] = text_term(1 - odd, 0)
    terms[1] = text_term(odd, 0)
    mate_copy(1).wait_recv()
    img_acc[2 - 2 * core] += mate_in[1].astype(F32)

    @pl.when(core_1)
    def _():
        mate_copy(2).wait_recv()
        img_acc[2] += mate_in[2].astype(F32)

    def take_over(kind, half, given):
        @pl.when(given)
        def _():
            over_copy(kind, half).wait_recv()
            at = slice(half * HALF, (half + 1) * HALF)
            img_acc[2 * kind, at, :] += over_in[kind, half].astype(F32)

    for half in (0, 1):
        take_over(0, half, is_odd)
        take_over(1, half, core_0 & (odd == 0))
        swap_out[half] = img_acc[2 - 2 * odd, half * HALF : (half + 1) * HALF, :].astype(BF16)
        start(swap_copy(half))
        back_copy(1, half).wait_recv()
        near_out[half] = (halves(terms[0])[half] + back_in[1, half].astype(F32)).astype(BF16)
        start(near_copy(half))
    for half in (0, 1):
        take_over(0, half, odd == 0)
        take_over(1, half, core_0 & is_odd)

    row_ref[...] = row_lse[pl.ds(own_at, 1), :] - (
        row_stat[2, pl.ds(own_at, 1), :] + row_got[1, 2, pl.ds(own_at, 1), :]
    )
    col_ref[...] = col_lse[0, pl.ds(z, 1), :] - col_lse[1, pl.ds(z, 1), :]

    def finish(source, summed):
        unit, inverse = unit_of(source)
        summed = factor * summed
        return (summed - unit * jnp.sum(unit * summed, axis=-1, keepdims=True)) * inverse

    for half in (0, 1):
        at = slice(half * HALF, (half + 1) * HALF)
        swap_copy(half).wait_recv()
        igrad_ref[at, :] = finish(img_ref[at, :], img_acc[2 * odd, at, :] + swap_in[half].astype(F32))

    for half in (0, 1):
        at = slice(half * HALF, (half + 1) * HALF)
        back_copy(0, half).wait_recv()
        near_copy(half).wait_recv()
        total = terms[1, at, :] + back_in[0, half].astype(F32) + near_in[half].astype(F32)
        tgrad_ref[at, :] = finish(txt_ref[at, :], total)

    for copy, given in sent:
        if given is None:
            copy.wait_send()
        else:
            pl.when(given)(copy.wait_send)


def hand_out(row_in, col_in, igrad_in, tgrad_in, row_ref, col_ref, igrad_ref, tgrad_ref, sems):
    copies = [
        pltpu.make_async_copy(src.at[pl.ds(n * 16, 16)], dst.at[pl.ds(n * 16, 16)], sems.at[k, n])
        for n in range(ROWS // 16)
        for k, (src, dst) in enumerate(((igrad_in, igrad_ref), (tgrad_in, tgrad_ref)))
    ]
    for copy in copies:
        copy.start()
    row_ref[...] = row_in[0]
    col_ref[...] = col_in[0]
    for copy in copies:
        copy.wait()


def on_device(image, text, positive, logit_scale, *, columns):
    width = image.shape[1]
    vmem = pl.BlockSpec(memory_space=pltpu.VMEM)
    dma = pltpu.SemaphoreType.DMA
    line, whole = pltpu.VMEM((1, ROWS), F32), pltpu.VMEM((ROWS, width), F32)
    found = pl.pallas_call(
        functools.partial(kernel, columns),
        out_shape=(line, line, whole, whole),
        in_specs=[pl.BlockSpec(memory_space=pltpu.SMEM), vmem, vmem, vmem],
        out_specs=(vmem,) * 4,
        scratch_shapes=[
            pltpu.VMEM((4, ROWS, width), BF16),
            pltpu.VMEM((8, ROWS, width), BF16),
            pltpu.VMEM((8, ROWS), F32),
            pltpu.VMEM((8, ROWS), F32),
            pltpu.VMEM((2, ROWS, ROWS), jnp.int32),
            pltpu.VMEM((4, 4 * ROWS, ROWS), F32),
            pltpu.VMEM((2, 4 * ROWS, 2 * ROWS), BF16),
            pltpu.VMEM((2, ROWS, width), F32),
            pltpu.VMEM((6, ROWS, width), F32),
            pltpu.VMEM((8, ROWS, ROWS), F32),
            pltpu.VMEM((8, ROWS, ROWS), F32),
            pltpu.VMEM((2, ROWS, ROWS), F32),
            pltpu.VMEM((3, 8, ROWS), F32),
            pltpu.VMEM((11, 3, 8, ROWS), F32),
            pltpu.VMEM((3, 8, ROWS), F32),
            pltpu.VMEM((5, 3, 8, ROWS), F32),
            pltpu.VMEM((8, ROWS), F32),
            pltpu.VMEM((2, 8, ROWS), F32),
            pltpu.VMEM((8, ROWS, ROWS), F32),
            pltpu.VMEM((2, 2, HALF, width), BF16),
            pltpu.VMEM((2, 2, HALF, width), BF16),
            pltpu.VMEM((2, HALF, width), BF16),
            pltpu.VMEM((2, HALF, width), BF16),
            pltpu.VMEM((3, ROWS, width), BF16),
            pltpu.VMEM((3, ROWS, width), BF16),
            pltpu.VMEM((2, 2, HALF, width), BF16),
            pltpu.VMEM((2, 2, HALF, width), BF16),
            pltpu.VMEM((2, HALF, width), BF16),
            pltpu.VMEM((2, HALF, width), BF16),
            dma((3, 2)), dma((3, 2)),
            dma((8,)), dma((8,)),
            dma((11,)), dma((11,)),
            dma((5,)), dma((5,)),
            dma((2, 2)), dma((2, 2)),
            dma((2,)), dma((2,)),
            dma((3,)), dma((3,)),
            dma((2, 2)), dma((2, 2)),
            dma((2,)), dma((2,)),
        ],
        compiler_params=pltpu.CompilerParams(collective_id=0, has_side_effects=True),
    )(logit_scale, image, text, positive)
    flat = jax.ShapeDtypeStruct((ROWS,), F32)
    anywhere = pl.BlockSpec(memory_space=pl.ANY)
    found = [pltpu.with_memory_space_constraint(x, pltpu.VMEM) for x in found]
    return pl.pallas_call(
        hand_out,
        out_shape=(flat, flat, *[jax.ShapeDtypeStruct((ROWS, width), F32)] * 2),
        in_specs=[vmem] * 4,
        out_specs=(vmem, vmem, anywhere, anywhere),
        scratch_shapes=[dma((2, ROWS // 16))],
    )(*found)


def solution(mesh):
    placed = (P(("blk", "rep"), None), P(("blk", "rep"), None), P("blk", "rep"), P())
    return jax.shard_map(
        functools.partial(on_device, columns=mesh.shape["blk"] // 4),
        mesh=mesh,
        in_specs=placed,
        out_specs=(
            P(("blk", "rep")),
            P(("blk", "rep")),
            P(("blk", "rep"), None),
            P(("blk", "rep"), None),
        ),
        check_vma=False,
    )
```

```python
import functools

import jax
import jax.numpy as jnp
from jax import lax
from jax.experimental import pallas as pl
from jax.experimental.pallas import tpu as pltpu
from jax.sharding import PartitionSpec as P

MESH = pl.DeviceIdType.MESH
F32 = jnp.float32
BF16 = jnp.bfloat16
ROWS = 128
HALF = 64
RING = 8
LOW = -1e30


def unit_of(values):
    widened = values.astype(F32)
    inverse = lax.rsqrt(jnp.sum(widened * widened, axis=-1, keepdims=True) + 1e-06)
    return widened * inverse, inverse


def dot(a, b, dims):
    return lax.dot_general(a, b, (dims, ((), ())), preferred_element_type=F32)


def halves(array):
    return [array[h * HALF : (h + 1) * HALF] for h in (0, 1)]


def kernel(
    columns,
    scale_ref, img_ref, txt_ref, pos_ref,
    row_ref, col_ref, igrad_ref, tgrad_ref,
    units, inverses, texts, images, pos_out, pos_in, pos_wide, scores, weights, terms, img_acc,
    peak, part, row_hit,
    row_stat, row_got, col_stat, col_got, row_lse, col_lse, row_wide,
    back_out, back_in, near_out, near_in, mate_out, mate_in, over_out, over_in, swap_out, swap_in,
    txt_send, txt_recv, pic_send, pic_recv, rs_send, rs_recv, cs_send, cs_recv,
    back_send, back_recv, near_send, near_recv, mate_send, mate_recv, over_send, over_recv, swap_send, swap_recv,
):
    blk, rep = lax.axis_index("blk"), lax.axis_index("rep")
    core = lax.rem(blk, 2)
    odd = lax.rem(lax.div(blk, 2), 2)
    col = lax.div(blk, 4)
    z = 2 * rep + odd
    tau = 1 - 2 * odd
    factor = scale_ref[...]

    def device(column, height, which):
        return (4 * column + 2 * lax.rem(height, 2) + which, lax.div(height, 2))

    def ring(by):
        return lax.rem(z + by + 2 * RING, RING)

    up, down = lax.rem(col + 1, columns), lax.rem(col + columns - 1, columns)
    pair_z, near_z, behind_z, far_z, ahead_z = (ring(s * tau) for s in (1, -1, -2, -3, 2))
    OWN, BEHIND, NEAR, FAR = 2 * odd, 2 * odd + 1, 2 - 2 * odd, 3 - 2 * odd
    is_odd = odd == 1
    other = 1 - core
    mate = device(col, z, other)
    pair = device(col, pair_z, core)
    near = device(col, near_z, core)
    behind = device(col, behind_z, core)
    ahead = device(col, ahead_z, core)

    def square(column):
        return [device(column, h, c) for h in (z, pair_z) for c in (core, other)]

    row_to = [(to, n) for n, to in enumerate(square(col)[1:])]
    row_to += [(to, 7 + n) for n, to in enumerate(square(up))]
    row_to += [(to, 3 + n) for n, to in enumerate(square(down))]
    col_to = [(near, 0)]
    col_to += [(device(col, ring(by), core), n) for by, n in ((3, 4), (-3, 3), (2, 2), (-2, 1))]

    barrier = pltpu.get_barrier_semaphore()
    friends = [to for to, _ in row_to + col_to]
    for friend in friends:
        pl.semaphore_signal(barrier, inc=1, device_id=friend, device_id_type=MESH)

    own_at, pair_at = 2 * odd + core, 2 * (1 - odd) + core
    mate_own_at, mate_pair_at = 2 * odd + other, 2 * (1 - odd) + other

    txt_unit, _ = unit_of(txt_ref[...])
    texts[OWN] = txt_unit.astype(BF16)

    pl.semaphore_wait(barrier, len(friends))

    sent = []

    def remote(src, dst, send, recv, to):
        return pltpu.make_async_remote_copy(
            src_ref=src, dst_ref=dst, send_sem=send, recv_sem=recv, device_id=to, device_id_type=MESH
        )

    def arrival(place, send, recv):
        return remote(place, place, send, recv, mate)

    def start(copy, given=None):
        if given is None:
            copy.start()
        else:
            pl.when(given)(copy.start)
        sent.append((copy, given))

    def arrived(copy, given=None):
        if given is None:
            copy.wait_recv()
        else:
            pl.when(given)(copy.wait_recv)

    def text_copy(kind, half):
        src, dst, to = ((OWN, OWN, near), (OWN, BEHIND, ahead), (NEAR, FAR, ahead))[kind]
        at = pl.ds(half * HALF, HALF)
        return remote(texts.at[src, at], texts.at[dst, at], txt_send.at[kind, half], txt_recv.at[kind, half], to)

    def text_arrival(kind, half):
        place = texts.at[(NEAR, BEHIND, FAR)[kind], pl.ds(half * HALF, HALF)]
        return arrival(place, txt_send.at[kind, half], txt_recv.at[kind, half])

    def image_copy(kind, src, dst, to):
        return remote(images.at[src], images.at[dst], pic_send.at[kind], pic_recv.at[kind], to)

    def image_arrival(kind, place):
        return arrival(images.at[place], pic_send.at[kind], pic_recv.at[kind])

    below = device(down, z, core)
    own_goes, pair_goes = own_at != 3, pair_at != 3
    mate_own_goes, mate_pair_goes = mate_own_at != 3, mate_pair_at != 3

    start(text_copy(0, 0))
    start(text_copy(0, 1))
    img_unit, _ = unit_of(img_ref[...])
    images[own_at] = img_unit.astype(BF16)
    pos_out[...] = jnp.broadcast_to(pos_ref[...].astype(F32), (8, ROWS))
    start(image_copy(0, own_at, own_at, pair))
    start(image_copy(1, own_at, own_at, mate))
    start(image_copy(3, own_at, own_at + 4, below), own_goes)
    start(text_copy(1, 0))
    start(text_copy(1, 1))
    start(remote(pos_out, pos_in, pic_send.at[7], pic_recv.at[7], pair))

    for kind, source in enumerate((img_ref, txt_ref)):
        unit, inverse = unit_of(source[...])
        units[kind] = unit
        inverses[kind] = jnp.broadcast_to(inverse, (ROWS, ROWS))
    lanes = lax.broadcasted_iota(jnp.int32, (ROWS, ROWS), 1)
    peak[...] = jnp.full(peak.shape, LOW, F32)
    part[...] = jnp.zeros(part.shape, F32)
    row_hit[...] = jnp.zeros(row_hit.shape, F32)
    row_stat[0] = jnp.full((8, ROWS), LOW, F32)
    row_stat[1] = jnp.zeros((8, ROWS), F32)
    row_stat[2] = jnp.zeros((8, ROWS), F32)
    col_stat[0] = jnp.full((8, ROWS), LOW, F32)
    col_stat[1] = jnp.zeros((8, ROWS), F32)
    col_stat[2] = jnp.zeros((8, ROWS), F32)

    for half in (0, 1):
        text_arrival(0, half).wait_recv()
        start(text_copy(2, half))
    image_arrival(0, pair_at).wait_recv()
    start(image_copy(4, pair_at, pair_at + 4, below), pair_goes)
    start(image_copy(2, pair_at, pair_at, mate))
    arrival(pos_in, pic_send.at[7], pic_recv.at[7]).wait_recv()

    def column(values):
        return jnp.broadcast_to(values, (ROWS, ROWS)).T.astype(jnp.int32)

    pos_wide[odd] = column(pos_out[0:1, :])
    pos_wide[1 - odd] = column(pos_in[0:1, :])

    image_arrival(1, mate_own_at).wait_recv()
    image_arrival(2, mate_pair_at).wait_recv()
    arrived(image_arrival(3, own_at + 4), own_goes)
    start(image_copy(5, own_at + 4, own_at + 4, mate), own_goes)
    arrived(image_arrival(4, pair_at + 4), pair_goes)
    start(image_copy(6, pair_at + 4, pair_at + 4, mate), pair_goes)
    arrived(image_arrival(5, mate_own_at + 4), mate_own_goes)
    arrived(image_arrival(6, mate_pair_at + 4), mate_pair_goes)

    def hits(parity, height):
        return pos_wide[parity] == lanes + ROWS * lax.div(height, 2)

    def window(parity):
        return images[pl.ds(2 * parity + core, 4)].reshape(4 * ROWS, -1)

    def score(which, parity, height):
        value = factor * dot(window(parity), texts[which], ((1,), (1,)))
        scores[which] = value
        highest = jnp.max(value, axis=0, keepdims=True)
        at = pl.ds(height, 1)
        col_stat[0, at, :] = highest
        col_stat[1, at, :] = jnp.sum(jnp.exp(value - highest), axis=0, keepdims=True)
        hit = jnp.where(hits(parity, height), value[:ROWS], 0.0)
        row_hit[parity] += hit
        col_stat[2, at, :] = jnp.sum(hit, axis=0, keepdims=True)
        blocks = value.reshape(4, ROWS, ROWS)
        here = pl.ds(2 * parity + core, 4)
        old = peak[here]
        top = jnp.maximum(old, blocks)
        part[here] = part[here] * jnp.exp(old - top) + jnp.exp(blocks - top)
        peak[here] = top

    def row_total(place):
        logs = (peak[place] + jnp.log(part[place])).T
        top = jnp.max(logs, axis=0, keepdims=True)
        row_stat[0, pl.ds(place, 1), :] = top
        row_stat[1, pl.ds(place, 1), :] = jnp.sum(jnp.exp(logs - top), axis=0, keepdims=True)

    score(OWN, odd, z)
    score(NEAR, 1 - odd, near_z)
    text_arrival(1, 0).wait_recv()
    text_arrival(1, 1).wait_recv()
    score(BEHIND, odd, behind_z)
    row_total(own_at + 2 * odd)
    row_total(own_at + 2 * odd + 1)
    row_stat[2, pl.ds(own_at, 1), :] = jnp.sum(row_hit[odd].T, axis=0, keepdims=True)
    text_arrival(2, 0).wait_recv()
    text_arrival(2, 1).wait_recv()
    score(FAR, 1 - odd, far_z)
    for n in range(4):
        row_total(pair_at + n)
    row_stat[2, pl.ds(pair_at, 1), :] = jnp.sum(row_hit[1 - odd].T, axis=0, keepdims=True)

    for to, n in row_to[3:]:
        start(remote(row_stat, row_got.at[n], rs_send.at[n], rs_recv.at[n], to))
    for to, n in col_to[1:] + col_to[:1]:
        start(remote(col_stat, col_got.at[n], cs_send.at[n], cs_recv.at[n], to))
    for to, n in row_to[:3]:
        start(remote(row_stat, row_got.at[n], rs_send.at[n], rs_recv.at[n], to))

    def total_of(found):
        top = functools.reduce(jnp.maximum, [f[0] for f in found])
        return top + jnp.log(functools.reduce(jnp.add, [f[1] * jnp.exp(f[0] - top) for f in found]))

    for n in range(11):
        arrival(row_got.at[n], rs_send.at[n], rs_recv.at[n]).wait_recv()
    found = [(row_stat[0], row_stat[1])] + [(row_got[n, 0], row_got[n, 1]) for n in range(3)]
    for n in range(4):
        found.append(
            tuple(
                jnp.concatenate([row_got[7 + n, k, 4:8, :], row_got[3 + n, k, 0:4, :]], axis=0) for k in (0, 1)
            )
        )
    row_lse[...] = total_of(found)
    for n in range(6):
        row_wide[core + n] = jnp.broadcast_to(row_lse[pl.ds(core + n, 1), :], (ROWS, ROWS)).T

    for n in range(5):
        arrival(col_got.at[n], cs_send.at[n], cs_recv.at[n]).wait_recv()
    found = [(col_stat[0], col_stat[1])] + [(col_got[n, 0], col_got[n, 1]) for n in range(5)]
    col_lse[0] = total_of(found)
    col_lse[1] = functools.reduce(jnp.add, [col_stat[2]] + [col_got[n, 2] for n in range(5)])

    def weigh(parity, side, height):
        value = scores[2 * parity + side]
        rows = row_wide[pl.ds(2 * parity + core, 4)].reshape(4 * ROWS, ROWS)
        weight = 0.5 * (jnp.exp(value - rows) + jnp.exp(value - col_lse[0, pl.ds(height, 1), :]))
        ones = jnp.where(hits(parity, height), 1.0, 0.0)
        weight = jnp.concatenate([weight[:ROWS] - ones, weight[ROWS:]], axis=0).astype(BF16)
        weights[parity, :, side * ROWS : (side + 1) * ROWS] = weight

    def text_term(parity, side):
        weight = weights[parity, :, side * ROWS : (side + 1) * ROWS]
        return dot(weight, window(parity), ((0,), (0,)))

    def image_term(parity, part_of):
        right = texts[2 * parity : 2 * parity + 2].reshape(2 * ROWS, -1)
        left = weights[parity, part_of * 2 * ROWS : (part_of + 1) * 2 * ROWS, :]
        return dot(left, right, ((1,), (0,))).reshape(2, ROWS, -1)

    def back_copy(kind, half):
        place = (kind, half)
        return remote(back_out.at[place], back_in.at[place], back_send.at[place], back_recv.at[place], behind)

    def near_copy(half):
        return remote(near_out.at[half], near_in.at[half], near_send.at[half], near_recv.at[half], near)

    def send_back(kind, value):
        for half, share in enumerate(halves(value)):
            back_out[kind, half] = share.astype(BF16)
            start(back_copy(kind, half))

    above = device(up, z, core)
    above_even = device(up, z, 0)
    core_0, core_1 = core == 0, core == 1

    def mate_copy(n):
        return remote(mate_out.at[n], mate_in.at[n], mate_send.at[n], mate_recv.at[n], mate)

    def over_copy(kind, half):
        place = (kind, half)
        to = above if kind == 0 else above_even
        return remote(over_out.at[place], over_in.at[place], over_send.at[place], over_recv.at[place], to)

    def swap_copy(half):
        return remote(swap_out.at[half], swap_in.at[half], swap_send.at[half], swap_recv.at[half], pair)

    weigh(1 - odd, 1, far_z)
    send_back(1, text_term(1 - odd, 1))
    weigh(1 - odd, 0, near_z)
    weigh(odd, 0, z)
    weigh(odd, 1, behind_z)
    img_acc[4:6] = image_term(1, 1)
    img_acc[2:4] = image_term(1, 0) + image_term(0, 1)
    mate_out[0] = img_acc[5 - 2 * core].astype(BF16)
    start(mate_copy(0))
    for half in (0, 1):
        over_out[1, half] = img_acc[5, half * HALF : (half + 1) * HALF, :].astype(BF16)
        start(over_copy(1, half), core_1 & (odd == 0))
    mate_copy(0).wait_recv()
    for half in (0, 1):
        at = slice(half * HALF, (half + 1) * HALF)
        over_out[0, half] = (img_acc[4, at, :] + mate_in[0, at, :].astype(F32)).astype(BF16)
        start(over_copy(0, half))
    for half in (0, 1):
        start(over_copy(1, half), core_1 & is_odd)
    send_back(0, text_term(odd, 1))
    img_acc[0:2] = image_term(0, 0)
    mate_out[1] = img_acc[1].astype(BF16)
    start(mate_copy(1))
    mate_out[2] = img_acc[3].astype(BF16)
    start(mate_copy(2), core_0)
    terms[0] = text_term(1 - odd, 0)
    terms[1] = text_term(odd, 0)
    mate_copy(1).wait_recv()
    img_acc[2 - 2 * core] += mate_in[1].astype(F32)

    @pl.when(core_1)
    def _():
        mate_copy(2).wait_recv()
        img_acc[2] += mate_in[2].astype(F32)

    def take_over(kind, half, given):
        @pl.when(given)
        def _():
            over_copy(kind, half).wait_recv()
            at = slice(half * HALF, (half + 1) * HALF)
            img_acc[2 * kind, at, :] += over_in[kind, half].astype(F32)

    for half in (0, 1):
        take_over(0, half, is_odd)
        take_over(1, half, core_0 & (odd == 0))
        swap_out[half] = img_acc[2 - 2 * odd, half * HALF : (half + 1) * HALF, :].astype(BF16)
        start(swap_copy(half))
        back_copy(1, half).wait_recv()
        near_out[half] = (halves(terms[0])[half] + back_in[1, half].astype(F32)).astype(BF16)
        start(near_copy(half))
    for half in (0, 1):
        take_over(0, half, odd == 0)
        take_over(1, half, core_0 & is_odd)

    row_ref[...] = row_lse[pl.ds(own_at, 1), :] - (
        row_stat[2, pl.ds(own_at, 1), :] + row_got[1, 2, pl.ds(own_at, 1), :]
    )
    col_ref[...] = col_lse[0, pl.ds(z, 1), :] - col_lse[1, pl.ds(z, 1), :]

    def finish(kind, at, summed):
        unit = units[kind, at, :]
        summed = factor * summed
        return (summed - unit * jnp.sum(unit * summed, axis=-1, keepdims=True)) * inverses[kind, at, 0:1]

    for half in (0, 1):
        at = slice(half * HALF, (half + 1) * HALF)
        swap_copy(half).wait_recv()
        igrad_ref[at, :] = finish(0, at, img_acc[2 * odd, at, :] + swap_in[half].astype(F32))

    for half in (0, 1):
        at = slice(half * HALF, (half + 1) * HALF)
        back_copy(0, half).wait_recv()
        total = terms[1, at, :] + back_in[0, half].astype(F32)
        near_copy(half).wait_recv()
        total += near_in[half].astype(F32)
        tgrad_ref[at, :] = finish(1, at, total)

    for copy, given in sent:
        if given is None:
            copy.wait_send()
        else:
            pl.when(given)(copy.wait_send)


def hand_out(row_in, col_in, igrad_in, tgrad_in, row_ref, col_ref, igrad_ref, tgrad_ref, sems):
    copies = [
        pltpu.make_async_copy(src.at[pl.ds(n * 16, 16)], dst.at[pl.ds(n * 16, 16)], sems.at[k, n])
        for n in range(ROWS // 16)
        for k, (src, dst) in enumerate(((igrad_in, igrad_ref), (tgrad_in, tgrad_ref)))
    ]
    for copy in copies:
        copy.start()
    row_ref[...] = row_in[0]
    col_ref[...] = col_in[0]
    for copy in copies:
        copy.wait()


def on_device(image, text, positive, logit_scale, *, columns):
    width = image.shape[1]
    vmem = pl.BlockSpec(memory_space=pltpu.VMEM)
    dma = pltpu.SemaphoreType.DMA
    line, whole = pltpu.VMEM((1, ROWS), F32), pltpu.VMEM((ROWS, width), F32)
    found = pl.pallas_call(
        functools.partial(kernel, columns),
        out_shape=(line, line, whole, whole),
        in_specs=[vmem] * 4,
        out_specs=(vmem,) * 4,
        scratch_shapes=[
            pltpu.VMEM((2, ROWS, width), F32),
            pltpu.VMEM((2, ROWS, ROWS), F32),
            pltpu.VMEM((4, ROWS, width), BF16),
            pltpu.VMEM((8, ROWS, width), BF16),
            pltpu.VMEM((8, ROWS), F32),
            pltpu.VMEM((8, ROWS), F32),
            pltpu.VMEM((2, ROWS, ROWS), jnp.int32),
            pltpu.VMEM((4, 4 * ROWS, ROWS), F32),
            pltpu.VMEM((2, 4 * ROWS, 2 * ROWS), BF16),
            pltpu.VMEM((2, ROWS, width), F32),
            pltpu.VMEM((6, ROWS, width), F32),
            pltpu.VMEM((8, ROWS, ROWS), F32),
            pltpu.VMEM((8, ROWS, ROWS), F32),
            pltpu.VMEM((2, ROWS, ROWS), F32),
            pltpu.VMEM((3, 8, ROWS), F32),
            pltpu.VMEM((11, 3, 8, ROWS), F32),
            pltpu.VMEM((3, 8, ROWS), F32),
            pltpu.VMEM((5, 3, 8, ROWS), F32),
            pltpu.VMEM((8, ROWS), F32),
            pltpu.VMEM((2, 8, ROWS), F32),
            pltpu.VMEM((8, ROWS, ROWS), F32),
            pltpu.VMEM((2, 2, HALF, width), BF16),
            pltpu.VMEM((2, 2, HALF, width), BF16),
            pltpu.VMEM((2, HALF, width), BF16),
            pltpu.VMEM((2, HALF, width), BF16),
            pltpu.VMEM((3, ROWS, width), BF16),
            pltpu.VMEM((3, ROWS, width), BF16),
            pltpu.VMEM((2, 2, HALF, width), BF16),
            pltpu.VMEM((2, 2, HALF, width), BF16),
            pltpu.VMEM((2, HALF, width), BF16),
            pltpu.VMEM((2, HALF, width), BF16),
            dma((3, 2)), dma((3, 2)),
            dma((8,)), dma((8,)),
            dma((11,)), dma((11,)),
            dma((5,)), dma((5,)),
            dma((2, 2)), dma((2, 2)),
            dma((2,)), dma((2,)),
            dma((3,)), dma((3,)),
            dma((2, 2)), dma((2, 2)),
            dma((2,)), dma((2,)),
        ],
        compiler_params=pltpu.CompilerParams(collective_id=0, has_side_effects=True),
    )(logit_scale.reshape(1, 1), image, text, positive)
    flat = jax.ShapeDtypeStruct((ROWS,), F32)
    anywhere = pl.BlockSpec(memory_space=pl.ANY)
    found = [pltpu.with_memory_space_constraint(x, pltpu.VMEM) for x in found]
    return pl.pallas_call(
        hand_out,
        out_shape=(flat, flat, *[jax.ShapeDtypeStruct((ROWS, width), F32)] * 2),
        in_specs=[vmem] * 4,
        out_specs=(vmem, vmem, anywhere, anywhere),
        scratch_shapes=[dma((2, ROWS // 16))],
    )(*found)


def solution(mesh):
    placed = (P(("blk", "rep"), None), P(("blk", "rep"), None), P("blk", "rep"), P())
    return jax.shard_map(
        functools.partial(on_device, columns=mesh.shape["blk"] // 4),
        mesh=mesh,
        in_specs=placed,
        out_specs=(
            P(("blk", "rep")),
            P(("blk", "rep")),
            P(("blk", "rep"), None),
            P(("blk", "rep"), None),
        ),
        check_vma=False,
    )
```
